512 devices in a mesh: slot: 8 (over x, core), tile: 64 (over y, z).
Axes of the slice: x: 4, y: 4, z: 16, core: 2. Of those that a mesh axis runs over, the one named last changes fastest.
Arguments:
- control: float32 [8, 4, 2, 1024, 512], P('slot', None, None, 'tile'), may hold values from -28 to 28
- background: bfloat16 [4, 2, 1024, 512], P(None, None, 'tile'), may hold values from -6 to 6
- self_weight: bfloat16 [512, 512], replicated, may hold values from -0.25 to 0.25
- neighbour_weight: bfloat16 [512, 512], replicated, may hold values from -0.25 to 0.25
- output_weight: bfloat16 [512, 512], replicated, may hold values from -0.25 to 0.25
- norm_gain: float32 [512], replicated, may hold values from 0.1 to 1.9
- readout: bfloat16 [512, 128], replicated, may hold values from -0.25 to 0.25
- error_weight: float32 [512], replicated, may hold values from 0.3 to 3
- report_owner: int32 [8, 2, 8192, 1], P('slot', None, 'tile'), may hold values from 0 to 63, as said below
- report_stencil: int32 [8, 2, 8192, 4], P('slot', None, 'tile'), may hold values from 0 to 31
- report_weights: bfloat16 [8, 2, 8192, 4], P('slot', None, 'tile'), may hold values from 0.049804688 to 1
- report_values: bfloat16 [8, 2, 8192, 128], P('slot', None, 'tile'), may hold values from -6 to 6
- report_precision: bfloat16 [8, 2, 8192], P('slot', None, 'tile'), may hold values from 0.049804688 to 0.5
Outputs:
- gradient: float32 [8, 4, 2, 1024, 512], P('slot', None, None, 'tile')
The draws below stay inside these ranges and needn't reach their ends.
Inputs may be any that keep to these rules, and one draw needn't show every extreme that they name: `report_owner`: within the rows of one device for one slot and step (aligned blocks of 128 rows) no owner tile is named more than 5 times; in every slot and step one owner tile is named exactly 5 times by every device of the slot. `report_stencil`: A cell of the owner tile, numbered latitude row * 16 + column within the tile.
All inputs are finite; a program needn't handle non-finite values.
Results may differ from the reference program's by a relative error of at most 0.006.
Values may be sent and summed in bfloat16 or wider, within the bound.
A program may use at most 64 MiB of HBM per device.

```python
import math
import jax
import jax.numpy as jnp
from jax import lax

C = 512
OBSV = 128
LAT_T = 2
LON_T = 16
MEMBERS = 4
STEPS = 2
CAP = 5
LON = 1024
OBS_DEV = 128
OBS_ROWS = 8192
N_SLOT = 8
N_TILE = 64


def draw_control(key, part):
    key_base, key_channel, key_cell = jax.random.split(jax.random.fold_in(key, 7), 3)
    full_shape = (N_SLOT, MEMBERS, LAT_T, LON, C)
    gaussian = jnp.clip(jax.random.normal(key_base, full_shape, jnp.float32), -4.0, 4.0)
    channel_scale = jnp.exp(jax.random.uniform(key_channel, (C,), jnp.float32, -1.15, 1.15))
    cell_scale = jnp.exp(jax.random.uniform(key_cell, (1, 1, LAT_T, LON, 1), jnp.float32, -0.7, 0.7))
    return gaussian * channel_scale * cell_scale


def draw_report_owner(key, part):
    key_heavy, key_rows = jax.random.split(jax.random.fold_in(key, 13))
    heavy_tiles = jax.random.randint(key_heavy, (N_SLOT * STEPS,), 0, N_TILE, dtype=jnp.int32)
    block_heavy = jnp.repeat(heavy_tiles, N_TILE)
    offset_pool = jnp.repeat(jnp.arange(1, N_TILE, dtype=jnp.int32), CAP)
    block_keys = jax.random.split(key_rows, N_SLOT * STEPS * N_TILE)

    def block_rows(block_key, heavy_tile):
        key_pick, key_order = jax.random.split(block_key)
        offsets = jax.random.permutation(key_pick, offset_pool)[:OBS_DEV - CAP]
        listed = jnp.concatenate([jnp.full((CAP,), heavy_tile, jnp.int32), (heavy_tile + offsets) % N_TILE])
        return jax.random.permutation(key_order, listed)
    owners = jax.vmap(block_rows)(block_keys, block_heavy)
    return owners.reshape(N_SLOT, STEPS, OBS_ROWS, 1).astype(jnp.int32)


def plant(entries, stream_key, least, high):
    longest = entries.shape.index(max(entries.shape))
    spots = []
    for shift in (0, 1):
        where = [jax.random.randint(jax.random.fold_in(stream_key, axis), (), 0, length) for axis, length in enumerate(entries.shape)]
        where[longest] = (where[longest] + shift) % entries.shape[longest]
        spots.append(tuple(where))
    return entries.at[spots[0]].set(least).at[spots[1]].set(high)


def shard_levels(stream_key, shape, cuts, low, largest):
    def one(position, parts):
        steps = jax.random.uniform(jax.random.fold_in(jax.random.fold_in(stream_key, 6), position), (parts,), jnp.float32, low / len(cuts), largest / len(cuts))
        return jnp.repeat(jnp.exp(steps), shape[position] // parts).reshape((-1,) + (1,) * (len(shape) - position - 1))

    factor_of = one(*cuts[0])
    for cut in cuts[1:]:
        factor_of = factor_of * one(*cut)
    return factor_of


def noise(own_key, dims, scale, bound, shards=(), held_as=jnp.bfloat16):
    entries = jax.random.normal(own_key, dims, jnp.float32) * scale
    if len(shards) > 0:
        entries = shard_levels(own_key, dims, shards, -0.22, 0.18) * entries
    return jnp.clip(entries, min=-bound, max=bound).astype(held_as)


def setup_inputs(seed: int = 0) -> dict:
    seeds = jax.random.split(jax.random.key(seed), 14)
    control = draw_control(jax.random.fold_in(seeds[13], 71), 0)
    background = noise(seeds[1], (MEMBERS, LAT_T, LON, C), 1.0, 6.0, ((2, 64),))
    self_weight = noise(seeds[2], (C, C), C ** -0.5, 0.25)
    neighbour_weight = noise(seeds[3], (C, C), C ** -0.5, 0.25)
    output_weight = noise(seeds[4], (C, C), C ** -0.5, 0.25)
    norm_gain = jnp.clip(1.0 + 0.18 * jax.random.normal(seeds[5], (C,), jnp.float32), 0.1, 1.9)
    readout = noise(seeds[6], (C, OBSV), C ** -0.5, 0.25)
    error_weight = jnp.clip(jnp.exp(jax.random.uniform(seeds[7], (C,), jnp.float32, math.log(0.3), math.log(3.0))), 0.3, 3.0)
    report_owner = draw_report_owner(jax.random.fold_in(seeds[13], 71), 0)
    report_stencil = plant(jax.random.randint(seeds[9], (N_SLOT, STEPS, OBS_ROWS, 4), 0, LAT_T * LON_T), jax.random.fold_in(seeds[9], 1), 0, (LAT_T * LON_T) - 1).astype(jnp.int32)
    report_weights = jnp.clip(0.049804688 + 0.9501953 * jax.random.uniform(seeds[10], (N_SLOT, STEPS, OBS_ROWS, 4), jnp.float32) ** shard_levels(seeds[10], (N_SLOT, STEPS, OBS_ROWS, 4), ((0, 8), (2, 64)), -0.2, 0.2), 0.049804688, 1.0).astype(jnp.bfloat16)
    report_values = noise(seeds[11], (N_SLOT, STEPS, OBS_ROWS, OBSV), 1.0, 6.0, ((0, 8), (2, 64)))
    report_precision = jnp.clip(jnp.exp(math.log(0.5) - 2.306499 * jax.random.uniform(seeds[12], (N_SLOT, STEPS, OBS_ROWS), jnp.float32) ** shard_levels(seeds[12], (N_SLOT, STEPS, OBS_ROWS), ((0, 8), (2, 64)), -0.2, 0.2)), 0.049804688, 0.5).astype(jnp.bfloat16)
    return {"control": control, "background": background, "self_weight": self_weight, "neighbour_weight": neighbour_weight, "output_weight": output_weight, "norm_gain": norm_gain, "readout": readout, "error_weight": error_weight, "report_owner": report_owner, "report_stencil": report_stencil, "report_weights": report_weights, "report_values": report_values, "report_precision": report_precision}


EPSILON = 1e-06

def matmul(operand, matrix):
    flattened = jnp.dot(operand.reshape(-1, operand.shape[-1]), matrix, preferred_element_type=jnp.float32)
    return flattened.reshape(operand.shape[:-1] + (matrix.shape[-1],))

def matmul_back(operand, matrix):
    flattened = jnp.dot(operand.reshape(-1, operand.shape[-1]), matrix.T, preferred_element_type=jnp.float32)
    return flattened.reshape(operand.shape[:-1] + (matrix.shape[0],))

def neighbour_sum(values):
    widened = values.astype(jnp.float32)
    zero_row = jnp.zeros_like(widened[:, :1])
    northern = jnp.concatenate([zero_row, widened[:, :-1]], axis=1)
    southern = jnp.concatenate([widened[:, 1:], zero_row], axis=1)
    return northern + southern + jnp.roll(widened, 1, axis=2) + jnp.roll(widened, -1, axis=2)

def normalize(current, norm_gain):
    inverse_rms = lax.rsqrt(lax.optimization_barrier(jnp.mean(current * current, axis=-1, keepdims=True)) + EPSILON)
    return ((current * inverse_rms * norm_gain).astype(jnp.bfloat16), inverse_rms)

def pre_activation(current, norm_gain, self_weight, neighbour_weight):
    normed, inverse_rms = normalize(current, norm_gain)
    mixed_mean = (0.25 * neighbour_sum(normed)).astype(jnp.bfloat16)
    return (inverse_rms, matmul(normed, self_weight) + matmul(mixed_mean, neighbour_weight))

def adjoint(current, inverse_rms, linear_sum, cotangent, norm_gain, self_weight, neighbour_weight, output_weight):
    grad_active = matmul_back(cotangent.astype(jnp.bfloat16), output_weight)
    sigmoid_value = jax.nn.sigmoid(linear_sum)
    grad_input = (grad_active * sigmoid_value * (1.0 + linear_sum * (1.0 - sigmoid_value))).astype(jnp.bfloat16)
    grad_mixed = matmul_back(grad_input, neighbour_weight).astype(jnp.bfloat16)
    grad_normed = matmul_back(grad_input, self_weight) + 0.25 * neighbour_sum(grad_mixed)
    scaled = norm_gain * grad_normed
    cubed_rms = inverse_rms * inverse_rms * inverse_rms
    return cotangent + inverse_rms * scaled - current * cubed_rms * lax.optimization_barrier(jnp.mean(current * scaled, axis=-1, keepdims=True))

def observe(current, owners, stencils, weights, values, precision, readout):
    members = current.shape[0]
    cell_count = LAT_T * LON_T
    flattened = current.astype(jnp.bfloat16).reshape(-1, C)
    readout_field = jnp.dot(flattened, readout, preferred_element_type=jnp.float32)
    readout_field = readout_field.reshape(members, LAT_T, N_TILE, LON_T, OBSV).transpose(0, 2, 1, 3, 4)
    readout_field = readout_field.reshape(members, N_TILE * cell_count, OBSV)
    cell_index = (owners * cell_count + stencils).astype(jnp.int32)
    stencil_weights = weights.astype(jnp.float32)
    predicted = lax.optimization_barrier(jnp.sum(readout_field[:, cell_index, :] * stencil_weights[None, :, :, None], axis=2))
    misfit = precision.astype(jnp.float32)[None, :, None] * (predicted - values.astype(jnp.float32)[None])

    def spread_member(member_misfit):
        weighted_terms = (member_misfit[:, None, :] * stencil_weights[:, :, None]).reshape(-1, OBSV)
        return jax.ops.segment_sum(weighted_terms, cell_index.reshape(-1), num_segments=N_TILE * cell_count)
    spread = jax.vmap(spread_member)(misfit).astype(jnp.bfloat16)
    spread = spread.reshape(members, N_TILE, LAT_T, LON_T, OBSV).transpose(0, 2, 1, 3, 4).reshape(-1, OBSV)
    pulled = jnp.dot(spread, readout.T, preferred_element_type=jnp.float32)
    return pulled.reshape(current.shape)

def slot_rows(table, slot, step_index):
    return lax.dynamic_index_in_dim(table, slot, 0, keepdims=False)[step_index]

def reference(control, background, self_weight, neighbour_weight, output_weight, norm_gain, readout, error_weight, report_owner, report_stencil, report_weights, report_values, report_precision):

    def slot_gradient(earlier_final, slot):
        current = lax.dynamic_index_in_dim(control, slot, 0, keepdims=False)
        later = jnp.minimum(slot + 1, N_SLOT - 1).astype(jnp.int32)
        following = lax.dynamic_index_in_dim(control, later, 0, keepdims=False)
        states = [current]
        kept = []
        for step_index in range(STEPS):
            inverse_rms, linear_sum = pre_activation(current, norm_gain, self_weight, neighbour_weight)
            kept.append((inverse_rms, linear_sum))
            current = current + matmul(jax.nn.silu(linear_sum).astype(jnp.bfloat16), output_weight)
            states.append(current)
        final_state = current.astype(jnp.bfloat16)
        own_misfit = error_weight * (states[0] - earlier_final.astype(jnp.float32))
        next_misfit = jnp.where(slot == N_SLOT - 1, 0.0, error_weight * (following - final_state.astype(jnp.float32)))
        pulls = []
        for step_index in range(STEPS):
            pulls.append(observe(states[step_index + 1], slot_rows(report_owner, slot, step_index), slot_rows(report_stencil, slot, step_index), slot_rows(report_weights, slot, step_index), slot_rows(report_values, slot, step_index), slot_rows(report_precision, slot, step_index), readout))
        cotangent = pulls[STEPS - 1] - next_misfit
        for step_index in reversed(range(STEPS)):
            inverse_rms, linear_sum = kept[step_index]
            cotangent = adjoint(states[step_index], inverse_rms, linear_sum, cotangent, norm_gain, self_weight, neighbour_weight, output_weight)
            if step_index > 0:
                cotangent = cotangent + pulls[step_index - 1]
        return (final_state, cotangent + own_misfit)
    unused_final, gradients = lax.scan(slot_gradient, background, jnp.arange(N_SLOT, dtype=jnp.int32))
    return gradients
```

```python
import functools

import jax
import jax.numpy as jnp
from jax import lax
from jax.experimental import pallas as pl
from jax.experimental.pallas import tpu as pltpu
from jax.sharding import PartitionSpec as P

MESH = pl.DeviceIdType.MESH
CAP = 5
EPSILON = 1e-06
FIELDS = 9
BLOCK = 16
F32 = jnp.float32
BF16 = jnp.bfloat16
HIGHEST = lax.Precision.HIGHEST


def iota(shape, dim):
    return lax.broadcasted_iota(jnp.int32, shape, dim)


def dot(a, b):
    return jnp.dot(a, b, preferred_element_type=F32)


def dot_back(a, b):
    return lax.dot_general(a, b, (((1,), (1,)), ((), ())), preferred_element_type=F32)


def dot_rows(a, b):
    return lax.dot_general(a, b, (((0,), (0,)), ((), ())), preferred_element_type=F32)


def slot_of_lane(lane):
    return lax.shift_right_logical(lane * 57, 9)


def pack_reports(steps, tiles, owner_ref, stencil_ref, weights_ref, values_ref, precision_ref, mt):
    rows = values_ref.shape[1]
    lane = iota((rows, 128), 1)
    row = iota((rows, 128), 0)
    lane_slot = slot_of_lane(lane)
    lane_field = lane - FIELDS * lane_slot
    spread_fields = jnp.where((row == lane_field) & (row < FIELDS), 1.0, 0.0).astype(BF16)
    place = iota((tiles * BLOCK, rows), 0)
    one_hots, operands = [], []
    mt[...] = jnp.zeros_like(mt)
    for k in range(steps):
        owner_row = owner_ref[k]
        mt[k, 0:4, :] = stencil_ref[k].astype(F32)
        mt[k, 4:8, :] = weights_ref[k].astype(F32)
        mt[k, 8:9, :] = precision_ref[0, k : k + 1, :].astype(F32)
        mt[k, 9:10, :] = owner_row.astype(F32)
        columns = mt[k].T
        owner_col = columns[:, 9:10].astype(jnp.int32)
        same = owner_col == owner_row
        rank_row = jnp.sum(jnp.where(same & (row < lane), 1, 0), axis=0, keepdims=True)
        rank_col = jnp.sum(jnp.where(same & (lane < row), 1, 0), axis=1, keepdims=True)
        meta = dot(columns.astype(BF16), spread_fields)
        meta = jnp.where(lane_slot == rank_col + CAP * k, meta, 0.0).astype(BF16)
        base = owner_row * BLOCK
        one_hots.append(jnp.where(place == base + (rank_row + CAP * k), 1.0, 0.0).astype(BF16))
        operands.append(values_ref[k])
        one_hots.append(jnp.where(place == base + CAP * steps, 1.0, 0.0).astype(BF16))
        operands.append(meta)
    return dot(jnp.concatenate(one_hots, axis=1), jnp.concatenate(operands, axis=0)).astype(BF16)


def report_operators(steps, tiles, arrived, cells):
    slots = CAP * steps
    meta = arrived[:, slots, :]
    lane_slot = slot_of_lane(iota((tiles, 128), 1))
    stacked = jnp.concatenate(
        [jnp.where(lane_slot == s, meta, 0.0) for s in range(slots)], axis=0
    ).astype(BF16)
    values = jnp.concatenate([arrived[:, s, :] for s in range(slots)], axis=0)
    lane = iota((128, 384), 0)
    column = iota((128, 384), 1)
    field = lane - FIELDS * slot_of_lane(lane)
    wanted = jnp.minimum(lax.shift_right_logical(column, 5), FIELDS - 1)
    expand = jnp.where((field == wanted) & (lane < FIELDS * slots), 1.0, 0.0).astype(BF16)
    expanded = dot(stacked, expand)
    cell = jnp.bitwise_and(iota((tiles * slots, 128), 1), cells - 1).astype(F32)
    table = jnp.where(expanded[:, 0:128] == cell, expanded[:, 128:256], 0.0)
    precision = expanded[:, 256:384]
    right = jnp.concatenate([precision * table, precision * values], axis=1)
    table = table.astype(BF16)
    high = right.astype(BF16)
    low = (right - high.astype(F32)).astype(BF16)
    r = iota((128, 128), 0)
    c = iota((128, 128), 1)
    fold = jnp.where(jnp.bitwise_and(r, cells - 1) == jnp.bitwise_and(c, cells - 1), 1.0, 0.0)
    member = lax.shift_right_logical(r, 5) == lax.shift_right_logical(c, 5)
    out = []
    for k in range(steps):
        part = slice(k * CAP * tiles, (k + 1) * CAP * tiles)
        both = dot_rows(table[part], high[part]) + dot_rows(table[part], low[part])
        both = jnp.dot(fold, both, precision=HIGHEST, preferred_element_type=F32)
        gram = jnp.dot(both[:, 0:128], fold, precision=HIGHEST, preferred_element_type=F32)
        out.append((jnp.where(member, gram, 0.0), both[:, 128:256]))
    return out


def kernel(
    slots,
    tiles,
    steps,
    control_ref,
    background_ref,
    self_ref,
    neighbour_ref,
    output_ref,
    gain_ref,
    readout_ref,
    error_ref,
    owner_ref,
    stencil_ref,
    weights_ref,
    values_ref,
    precision_ref,
    out_ref,
    mt,
    send_buf,
    recv_buf,
    arrived,
    edge_send,
    edge_recv,
    own,
    west,
    east,
    next_control,
    final_send,
    final_recv,
    report_send_sem,
    report_recv_sem,
    edge_send_sem,
    edge_recv_sem,
    state_send_sem,
    state_recv_sem,
):
    slot = lax.axis_index("slot")
    tile = lax.axis_index("tile")
    east_tile, west_tile = lax.rem(tile + 1, tiles), lax.rem(tile + tiles - 1, tiles)
    next_slot, last_slot = lax.rem(slot + 1, slots), lax.rem(slot + slots - 1, slots)
    rows, channels = control_ref.shape
    groups = rows // BLOCK

    barrier = pltpu.get_barrier_semaphore()

    @pl.loop(1, tiles)
    def _(distance):
        peer = lax.rem(tile + distance, tiles)
        pl.semaphore_signal(barrier, inc=1, device_id=(slot, peer), device_id_type=MESH)

    for peer in (next_slot, last_slot):
        pl.semaphore_signal(barrier, inc=1, device_id=(peer, tile), device_id_type=MESH)

    def edge_copy(turn, side):
        return pltpu.make_async_remote_copy(
            src_ref=edge_send.at[turn, side],
            dst_ref=edge_recv.at[turn, side],
            send_sem=edge_send_sem.at[turn, side],
            recv_sem=edge_recv_sem.at[turn, side],
            device_id=(slot, east_tile if side == 0 else west_tile),
            device_id_type=MESH,
        )

    def set_edges(turn, rounded):
        own[...] = rounded.astype(F32).reshape(groups, BLOCK, channels)
        edge_send[turn, 0] = own[:, BLOCK - 1, :].astype(BF16)
        edge_send[turn, 1] = own[:, 0, :].astype(BF16)

    def send_edges(turn):
        edge_copy(turn, 0).start()
        edge_copy(turn, 1).start()

    def neighbours(turn):
        whole = own[...].reshape(rows, channels)
        west[...] = pltpu.roll(whole, 1, 0).reshape(groups, BLOCK, channels)
        east[...] = pltpu.roll(whole, rows - 1, 0).reshape(groups, BLOCK, channels)
        swapped = jnp.concatenate(
            [whole[BLOCK * (g ^ 1) : BLOCK * (g ^ 1) + BLOCK] for g in range(groups)], axis=0
        )
        edge_copy(turn, 0).wait_recv()
        edge_copy(turn, 1).wait_recv()
        west[:, 0, :] = edge_recv[turn, 0].astype(F32)
        east[:, BLOCK - 1, :] = edge_recv[turn, 1].astype(F32)
        return (
            swapped
            + west[...].reshape(rows, channels)
            + east[...].reshape(rows, channels)
        )

    gain = gain_ref[...]

    def normalize(current):
        inverse_rms = lax.rsqrt(jnp.mean(current * current, axis=-1, keepdims=True) + EPSILON)
        return (current * inverse_rms * gain).astype(BF16), inverse_rms

    control_copy = pltpu.make_async_remote_copy(
        src_ref=control_ref,
        dst_ref=next_control,
        send_sem=state_send_sem.at[0],
        recv_sem=state_recv_sem.at[0],
        device_id=(last_slot, tile),
        device_id_type=MESH,
    )
    final_copy = pltpu.make_async_remote_copy(
        src_ref=final_send,
        dst_ref=final_recv,
        send_sem=state_send_sem.at[1],
        recv_sem=state_recv_sem.at[1],
        device_id=(next_slot, tile),
        device_id_type=MESH,
    )

    current = control_ref[...]
    normed, inverse_rms = normalize(current)
    set_edges(0, normed)
    packed = pack_reports(
        steps, tiles, owner_ref, stencil_ref, weights_ref, values_ref, precision_ref, mt
    )
    send_buf[...] = packed.reshape(tiles, BLOCK, 128)
    pl.semaphore_wait(barrier, tiles + 1)
    send_edges(0)

    @pl.loop(1, tiles)
    def _(distance):
        peer = lax.rem(tile + distance, tiles)
        pltpu.make_async_remote_copy(
            src_ref=send_buf.at[peer],
            dst_ref=recv_buf.at[tile],
            send_sem=report_send_sem,
            recv_sem=report_recv_sem,
            device_id=(slot, peer),
            device_id_type=MESH,
        ).start()

    control_copy.start()
    recv_buf[pl.ds(tile, 1)] = send_buf[pl.ds(tile, 1)]

    states, kept, fields = [], [], []
    for k in range(steps):
        if k > 0:
            normed, inverse_rms = normalize(current)
            set_edges(k, normed)
            send_edges(k)
        linear = dot(normed, self_ref[...])
        mixed = (0.25 * neighbours(k)).astype(BF16)
        linear = linear + dot(mixed, neighbour_ref[...])
        sigmoid = 1.0 / (1.0 + jnp.exp(-linear))
        states.append(current)
        kept.append((inverse_rms, sigmoid * (1.0 + linear * (1.0 - sigmoid))))
        current = current + dot((linear * sigmoid).astype(BF16), output_ref[...])
        fields.append(dot(current.astype(BF16), readout_ref[...]))
    final = current.astype(BF16)
    final_send[...] = final
    final_copy.start()

    others = pl.ds(0, tiles - 1)
    everyone = pltpu.make_async_remote_copy(
        src_ref=send_buf.at[others],
        dst_ref=recv_buf.at[others],
        send_sem=report_send_sem,
        recv_sem=report_recv_sem,
        device_id=(slot, east_tile),
        device_id_type=MESH,
    )
    everyone.wait_recv()
    arrived[...] = recv_buf[...].astype(F32)
    pulls = []
    for (gram, offset), field in zip(report_operators(steps, tiles, arrived, 2 * BLOCK), fields):
        spread = jnp.dot(gram, field, precision=HIGHEST, preferred_element_type=F32) - offset
        pulls.append(dot_back(spread.astype(BF16), readout_ref[...]))

    error = error_ref[...]
    control_copy.wait_recv()
    next_misfit = error * (next_control[...] - final.astype(F32))
    cotangent = pulls[-1] - jnp.where(slot == slots - 1, 0.0, next_misfit)
    for k in reversed(range(steps)):
        turn = 2 * steps - 1 - k
        inverse_rms, slope = kept[k]
        back = dot_back(cotangent.astype(BF16), output_ref[...])
        back = (back * slope).astype(BF16)
        set_edges(turn, dot_back(back, neighbour_ref[...]).astype(BF16))
        send_edges(turn)
        own_part = dot_back(back, self_ref[...])
        scaled = gain * (own_part + 0.25 * neighbours(turn))
        mean = jnp.mean(states[k] * scaled, axis=-1, keepdims=True)
        cubed = inverse_rms * inverse_rms * inverse_rms
        cotangent = cotangent + inverse_rms * scaled - states[k] * (cubed * mean)
        if k > 0:
            cotangent = cotangent + pulls[k - 1]

    final_copy.wait_recv()
    previous = jnp.where(slot == 0, background_ref[...].astype(F32), final_recv[...].astype(F32))
    out_ref[...] = cotangent + error * (control_ref[...] - previous)

    everyone.wait_send()
    for turn in range(2 * steps):
        edge_copy(turn, 0).wait_send()
        edge_copy(turn, 1).wait_send()
    control_copy.wait_send()
    final_copy.wait_send()


def solution(mesh):
    slots, tiles = mesh.shape["slot"], mesh.shape["tile"]

    def per_device(
        control,
        background,
        self_weight,
        neighbour_weight,
        output_weight,
        norm_gain,
        readout,
        error_weight,
        report_owner,
        report_stencil,
        report_weights,
        report_values,
        report_precision,
    ):
        channels = control.shape[-1]
        rows = control.size // channels
        steps = report_values.shape[1]
        groups = rows // BLOCK
        edges = (2 * steps, 2, groups, channels)
        block = (groups, BLOCK, channels)
        message = (tiles, BLOCK, 128)
        out = pl.pallas_call(
            functools.partial(kernel, slots, tiles, steps),
            out_shape=jax.ShapeDtypeStruct((rows, channels), F32),
            in_specs=[pl.BlockSpec(memory_space=pltpu.VMEM)] * 13,
            out_specs=pl.BlockSpec(memory_space=pltpu.VMEM),
            scratch_shapes=[
                pltpu.VMEM((steps, 128, 128), F32),
                pltpu.VMEM(message, BF16),
                pltpu.VMEM(message, BF16),
                pltpu.VMEM(message, F32),
                pltpu.VMEM(edges, BF16),
                pltpu.VMEM(edges, BF16),
                pltpu.VMEM(block, F32),
                pltpu.VMEM(block, F32),
                pltpu.VMEM(block, F32),
                pltpu.VMEM((rows, channels), F32),
                pltpu.VMEM((rows, channels), BF16),
                pltpu.VMEM((rows, channels), BF16),
                pltpu.SemaphoreType.DMA,
                pltpu.SemaphoreType.DMA,
                pltpu.SemaphoreType.DMA((2 * steps, 2)),
                pltpu.SemaphoreType.DMA((2 * steps, 2)),
                pltpu.SemaphoreType.DMA((2,)),
                pltpu.SemaphoreType.DMA((2,)),
            ],
            compiler_params=pltpu.CompilerParams(collective_id=0, has_side_effects=True),
        )(
            control.reshape(rows, channels),
            background.reshape(rows, channels),
            self_weight,
            neighbour_weight,
            output_weight,
            norm_gain.reshape(1, channels),
            readout,
            error_weight.reshape(1, channels),
            report_owner[0].transpose(0, 2, 1),
            report_stencil[0].transpose(0, 2, 1),
            report_weights[0].transpose(0, 2, 1),
            report_values[0],
            report_precision,
        )
        return out.reshape(control.shape)

    in_specs = (
        P("slot", None, None, "tile", None),
        P(None, None, "tile", None),
        P(),
        P(),
        P(),
        P(),
        P(),
        P(),
        P("slot", None, "tile", None),
        P("slot", None, "tile", None),
        P("slot", None, "tile", None),
        P("slot", None, "tile", None),
        P("slot", None, "tile"),
    )
    out_specs = P("slot", None, None, "tile", None)
    return jax.shard_map(
        per_device, mesh=mesh, in_specs=in_specs, out_specs=out_specs, check_vma=False
    )
```

```python
import functools

import jax
import jax.numpy as jnp
from jax import lax
from jax.experimental import pallas as pl
from jax.experimental.pallas import tpu as pltpu
from jax.sharding import PartitionSpec as P

MESH = pl.DeviceIdType.MESH
CAP = 5
EPSILON = 1e-06
FIELDS = 9
BLOCK = 16
SENT = 12
F32 = jnp.float32
BF16 = jnp.bfloat16
HIGHEST = lax.Precision.HIGHEST


def iota(shape, dim):
    return lax.broadcasted_iota(jnp.int32, shape, dim)


def dot(a, b):
    return jnp.dot(a, b, preferred_element_type=F32)


def dot_back(a, b):
    return lax.dot_general(a, b, (((1,), (1,)), ((), ())), preferred_element_type=F32)


def dot_rows(a, b):
    return lax.dot_general(a, b, (((0,), (0,)), ((), ())), preferred_element_type=F32)


def slot_of_lane(lane):
    return lax.shift_right_logical(lane * 57, 9)


def farthest_first(tile, tiles, ring, send):
    outer = tiles // ring
    line, place = tile // ring, lax.rem(tile, ring)

    def one(turn, across):
        step = (turn + 1) // 2
        along = jnp.where(lax.rem(turn, 2) == 1, ring // 2 + step, ring // 2 - step)
        send(lax.rem(line + across, outer) * ring + lax.rem(place + along, ring))

    @pl.loop(0, ring - 1)
    def _(turn):
        for across in range(outer):
            one(turn, (across + outer // 2) % outer)

    for across in range(1, outer):
        send(lax.rem(line + across, outer) * ring + place)


def pack_reports(steps, tiles, owner_ref, stencil_ref, weights_ref, values_ref, precision_ref, mt):
    rows = values_ref.shape[1]
    lane = iota((rows, 128), 1)
    row = iota((rows, 128), 0)
    lane_slot = slot_of_lane(lane)
    lane_field = lane - FIELDS * lane_slot
    spread_fields = jnp.where((row == lane_field) & (row < FIELDS), 1.0, 0.0).astype(BF16)
    place = iota((tiles * BLOCK, rows), 0)
    one_hots, operands = [], []
    mt[...] = jnp.zeros_like(mt)
    for k in range(steps):
        owner_row = owner_ref[k]
        mt[k, 0:4, :] = stencil_ref[k].astype(F32)
        mt[k, 4:8, :] = weights_ref[k].astype(F32)
        mt[k, 8:9, :] = precision_ref[0, k : k + 1, :].astype(F32)
        mt[k, 9:10, :] = owner_row.astype(F32)
        columns = mt[k].T
        owner_col = columns[:, 9:10].astype(jnp.int32)
        same = owner_col == owner_row
        rank_row = jnp.sum(jnp.where(same & (row < lane), 1, 0), axis=0, keepdims=True)
        rank_col = jnp.sum(jnp.where(same & (lane < row), 1, 0), axis=1, keepdims=True)
        meta = dot(columns.astype(BF16), spread_fields)
        meta = jnp.where(lane_slot == rank_col + CAP * k, meta, 0.0).astype(BF16)
        base = owner_row * BLOCK
        one_hots.append(jnp.where(place == base + (rank_row + CAP * k), 1.0, 0.0).astype(BF16))
        operands.append(values_ref[k])
        one_hots.append(jnp.where(place == base + CAP * steps, 1.0, 0.0).astype(BF16))
        operands.append(meta)
    return dot(jnp.concatenate(one_hots, axis=1), jnp.concatenate(operands, axis=0)).astype(BF16)


def report_operators(steps, tiles, arrived, cells):
    slots = CAP * steps
    meta = arrived[:, slots, :]
    lane_slot = slot_of_lane(iota((tiles, 128), 1))
    stacked = jnp.concatenate(
        [jnp.where(lane_slot == s, meta, 0.0) for s in range(slots)], axis=0
    ).astype(BF16)
    values = jnp.concatenate([arrived[:, s, :] for s in range(slots)], axis=0)
    lane = iota((128, 384), 0)
    column = iota((128, 384), 1)
    field = lane - FIELDS * slot_of_lane(lane)
    wanted = jnp.minimum(lax.shift_right_logical(column, 5), FIELDS - 1)
    expand = jnp.where((field == wanted) & (lane < FIELDS * slots), 1.0, 0.0).astype(BF16)
    expanded = dot(stacked, expand)
    cell = jnp.bitwise_and(iota((tiles * slots, 128), 1), cells - 1).astype(F32)
    table = jnp.where(expanded[:, 0:128] == cell, expanded[:, 128:256], 0.0)
    precision = expanded[:, 256:384]
    right = jnp.concatenate([precision * table, precision * values], axis=1)
    table = table.astype(BF16)
    high = right.astype(BF16)
    low = (right - high.astype(F32)).astype(BF16)
    r = iota((128, 128), 0)
    c = iota((128, 128), 1)
    fold = jnp.where(jnp.bitwise_and(r, cells - 1) == jnp.bitwise_and(c, cells - 1), 1.0, 0.0)
    member = lax.shift_right_logical(r, 5) == lax.shift_right_logical(c, 5)
    out = []
    for k in range(steps):
        part = slice(k * CAP * tiles, (k + 1) * CAP * tiles)
        both = dot_rows(table[part], high[part]) + dot_rows(table[part], low[part])
        both = jnp.dot(fold, both, precision=HIGHEST, preferred_element_type=F32)
        gram = jnp.dot(both[:, 0:128], fold, precision=HIGHEST, preferred_element_type=F32)
        out.append((jnp.where(member, gram, 0.0), both[:, 128:256]))
    return out


def kernel(
    slots,
    tiles,
    ring,
    steps,
    control_hbm,
    background_hbm,
    self_hbm,
    neighbour_hbm,
    output_hbm,
    gain_hbm,
    readout_hbm,
    error_hbm,
    owner_hbm,
    stencil_hbm,
    weights_hbm,
    values_hbm,
    precision_hbm,
    out_ref,
    control_ref,
    background_ref,
    self_ref,
    neighbour_ref,
    output_ref,
    gain_ref,
    readout_ref,
    error_ref,
    owner_ref,
    stencil_ref,
    weights_ref,
    values_ref,
    precision_ref,
    fetch_sem,
    mt,
    send_buf,
    recv_buf,
    arrived,
    edge_send,
    edge_recv,
    own,
    west,
    east,
    next_control,
    final_send,
    final_recv,
    report_send_sem,
    report_recv_sem,
    edge_send_sem,
    edge_recv_sem,
    state_send_sem,
    state_recv_sem,
):
    slot = lax.axis_index("slot")
    tile = lax.axis_index("tile")
    east_tile, west_tile = lax.rem(tile + 1, tiles), lax.rem(tile + tiles - 1, tiles)
    next_slot, last_slot = lax.rem(slot + 1, slots), lax.rem(slot + slots - 1, slots)
    rows, channels = control_ref.shape
    groups = rows // BLOCK

    fetches = [
        pltpu.make_async_copy(source, target, fetch_sem.at[i])
        for i, (source, target) in enumerate(
            (
                (control_hbm, control_ref),
                (gain_hbm, gain_ref),
                (owner_hbm, owner_ref),
                (stencil_hbm, stencil_ref),
                (weights_hbm, weights_ref),
                (precision_hbm, precision_ref),
                (values_hbm, values_ref),
                (self_hbm, self_ref),
                (neighbour_hbm, neighbour_ref),
                (output_hbm, output_ref),
                (readout_hbm, readout_ref),
                (error_hbm, error_ref),
                (background_hbm, background_ref),
            )
        )
    ]
    barrier = pltpu.get_barrier_semaphore()

    def greet(peer):
        pl.semaphore_signal(barrier, inc=1, device_id=(slot, peer), device_id_type=MESH)

    farthest_first(tile, tiles, ring, greet)
    for peer in (next_slot, last_slot):
        pl.semaphore_signal(barrier, inc=1, device_id=(peer, tile), device_id_type=MESH)

    for fetch in fetches:
        fetch.start()

    def edge_copy(turn, side):
        return pltpu.make_async_remote_copy(
            src_ref=edge_send.at[turn, side],
            dst_ref=edge_recv.at[turn, side],
            send_sem=edge_send_sem.at[turn, side],
            recv_sem=edge_recv_sem.at[turn, side],
            device_id=(slot, east_tile if side == 0 else west_tile),
            device_id_type=MESH,
        )

    def set_edges(turn, rounded):
        own[...] = rounded.astype(F32).reshape(groups, BLOCK, channels)
        edge_send[turn, 0] = own[:, BLOCK - 1, :].astype(BF16)
        edge_send[turn, 1] = own[:, 0, :].astype(BF16)

    def send_edges(turn):
        edge_copy(turn, 0).start()
        edge_copy(turn, 1).start()

    def neighbours(turn):
        whole = own[...].reshape(rows, channels)
        west[...] = pltpu.roll(whole, 1, 0).reshape(groups, BLOCK, channels)
        east[...] = pltpu.roll(whole, rows - 1, 0).reshape(groups, BLOCK, channels)
        swapped = jnp.concatenate(
            [whole[BLOCK * (g ^ 1) : BLOCK * (g ^ 1) + BLOCK] for g in range(groups)], axis=0
        )
        edge_copy(turn, 0).wait_recv()
        edge_copy(turn, 1).wait_recv()
        west[:, 0, :] = edge_recv[turn, 0].astype(F32)
        east[:, BLOCK - 1, :] = edge_recv[turn, 1].astype(F32)
        return (
            swapped
            + west[...].reshape(rows, channels)
            + east[...].reshape(rows, channels)
        )

    for fetch in fetches:
        fetch.wait()
    gain = gain_ref[...]

    def normalize(current):
        inverse_rms = lax.rsqrt(jnp.mean(current * current, axis=-1, keepdims=True) + EPSILON)
        return (current * inverse_rms * gain).astype(BF16), inverse_rms

    control_copy = pltpu.make_async_remote_copy(
        src_ref=control_ref,
        dst_ref=next_control,
        send_sem=state_send_sem.at[0],
        recv_sem=state_recv_sem.at[0],
        device_id=(last_slot, tile),
        device_id_type=MESH,
    )
    final_copy = pltpu.make_async_remote_copy(
        src_ref=final_send,
        dst_ref=final_recv,
        send_sem=state_send_sem.at[1],
        recv_sem=state_recv_sem.at[1],
        device_id=(next_slot, tile),
        device_id_type=MESH,
    )

    current = control_ref[...]
    normed, inverse_rms = normalize(current)
    set_edges(0, normed)
    packed = pack_reports(
        steps, tiles, owner_ref, stencil_ref, weights_ref, values_ref, precision_ref, mt
    )
    send_buf[...] = packed.reshape(tiles, BLOCK, 128)
    pl.semaphore_wait(barrier, tiles + 1)
    send_edges(0)

    def send_reports(peer):
        pltpu.make_async_remote_copy(
            src_ref=send_buf.at[peer, 0:SENT],
            dst_ref=recv_buf.at[tile, 0:SENT],
            send_sem=report_send_sem,
            recv_sem=report_recv_sem,
            device_id=(slot, peer),
            device_id_type=MESH,
        ).start()

    farthest_first(tile, tiles, ring, send_reports)
    control_copy.start()
    recv_buf[pl.ds(tile, 1)] = send_buf[pl.ds(tile, 1)]

    states, kept, fields = [], [], []
    for k in range(steps):
        if k > 0:
            normed, inverse_rms = normalize(current)
            set_edges(k, normed)
            send_edges(k)
        linear = dot(normed, self_ref[...])
        mixed = (0.25 * neighbours(k)).astype(BF16)
        linear = linear + dot(mixed, neighbour_ref[...])
        sigmoid = 1.0 / (1.0 + jnp.exp(-linear))
        states.append(current)
        kept.append((inverse_rms, sigmoid * (1.0 + linear * (1.0 - sigmoid))))
        current = current + dot((linear * sigmoid).astype(BF16), output_ref[...])
        fields.append(dot(current.astype(BF16), readout_ref[...]))
    final = current.astype(BF16)
    final_send[...] = final
    final_copy.start()

    others = pl.ds(0, tiles - 1)
    everyone = pltpu.make_async_remote_copy(
        src_ref=send_buf.at[others, 0:SENT],
        dst_ref=recv_buf.at[others, 0:SENT],
        send_sem=report_send_sem,
        recv_sem=report_recv_sem,
        device_id=(slot, east_tile),
        device_id_type=MESH,
    )
    everyone.wait_recv()
    arrived[...] = recv_buf[...].astype(F32)
    pulls = []
    for (gram, offset), field in zip(report_operators(steps, tiles, arrived, 2 * BLOCK), fields):
        spread = jnp.dot(gram, field, precision=HIGHEST, preferred_element_type=F32) - offset
        pulls.append(dot_back(spread.astype(BF16), readout_ref[...]))

    error = error_ref[...]
    control_copy.wait_recv()
    next_misfit = error * (next_control[...] - final.astype(F32))
    cotangent = pulls[-1] - jnp.where(slot == slots - 1, 0.0, next_misfit)
    for k in reversed(range(steps)):
        turn = 2 * steps - 1 - k
        inverse_rms, slope = kept[k]
        back = dot_back(cotangent.astype(BF16), output_ref[...])
        back = (back * slope).astype(BF16)
        set_edges(turn, dot_back(back, neighbour_ref[...]).astype(BF16))
        send_edges(turn)
        own_part = dot_back(back, self_ref[...])
        scaled = gain * (own_part + 0.25 * neighbours(turn))
        mean = jnp.mean(states[k] * scaled, axis=-1, keepdims=True)
        cubed = inverse_rms * inverse_rms * inverse_rms
        cotangent = cotangent + inverse_rms * scaled - states[k] * (cubed * mean)
        if k > 0:
            cotangent = cotangent + pulls[k - 1]

    final_copy.wait_recv()
    previous = jnp.where(slot == 0, background_ref[...].astype(F32), final_recv[...].astype(F32))
    out_ref[...] = cotangent + error * (control_ref[...] - previous)

    everyone.wait_send()
    for turn in range(2 * steps):
        edge_copy(turn, 0).wait_send()
        edge_copy(turn, 1).wait_send()
    control_copy.wait_send()
    final_copy.wait_send()


def solution(mesh):
    slots, tiles = mesh.shape["slot"], mesh.shape["tile"]

    def per_device(
        control,
        background,
        self_weight,
        neighbour_weight,
        output_weight,
        norm_gain,
        readout,
        error_weight,
        report_owner,
        report_stencil,
        report_weights,
        report_values,
        report_precision,
    ):
        channels = control.shape[-1]
        rows = control.size // channels
        steps = report_values.shape[1]
        groups = rows // BLOCK
        ring = 16 if tiles % 16 == 0 else tiles
        edges = (2 * steps, 2, groups, channels)
        block = (groups, BLOCK, channels)
        message = (tiles, BLOCK, 128)
        operands = (
            control.reshape(rows, channels),
            background.reshape(rows, channels),
            self_weight,
            neighbour_weight,
            output_weight,
            norm_gain.reshape(1, channels),
            readout,
            error_weight.reshape(1, channels),
            report_owner[0].transpose(0, 2, 1),
            report_stencil[0].transpose(0, 2, 1),
            report_weights[0].transpose(0, 2, 1),
            report_values[0],
            report_precision,
        )
        out = pl.pallas_call(
            functools.partial(kernel, slots, tiles, ring, steps),
            out_shape=jax.ShapeDtypeStruct((rows, channels), F32),
            in_specs=[pl.BlockSpec(memory_space=pl.ANY)] * len(operands),
            out_specs=pl.BlockSpec(memory_space=pltpu.VMEM),
            scratch_shapes=[
                *[pltpu.VMEM(operand.shape, operand.dtype) for operand in operands],
                pltpu.SemaphoreType.DMA((len(operands),)),
                pltpu.VMEM((steps, 128, 128), F32),
                pltpu.VMEM(message, BF16),
                pltpu.VMEM(message, BF16),
                pltpu.VMEM(message, F32),
                pltpu.VMEM(edges, BF16),
                pltpu.VMEM(edges, BF16),
                pltpu.VMEM(block, F32),
                pltpu.VMEM(block, F32),
                pltpu.VMEM(block, F32),
                pltpu.VMEM((rows, channels), F32),
                pltpu.VMEM((rows, channels), BF16),
                pltpu.VMEM((rows, channels), BF16),
                pltpu.SemaphoreType.DMA,
                pltpu.SemaphoreType.DMA,
                pltpu.SemaphoreType.DMA((2 * steps, 2)),
                pltpu.SemaphoreType.DMA((2 * steps, 2)),
                pltpu.SemaphoreType.DMA((2,)),
                pltpu.SemaphoreType.DMA((2,)),
            ],
            compiler_params=pltpu.CompilerParams(collective_id=0, has_side_effects=True),
        )(*operands)
        return out.reshape(control.shape)

    in_specs = (
        P("slot", None, None, "tile", None),
        P(None, None, "tile", None),
        P(),
        P(),
        P(),
        P(),
        P(),
        P(),
        P("slot", None, "tile", None),
        P("slot", None, "tile", None),
        P("slot", None, "tile", None),
        P("slot", None, "tile", None),
        P("slot", None, "tile"),
    )
    out_specs = P("slot", None, None, "tile", None)
    return jax.shard_map(
        per_device, mesh=mesh, in_specs=in_specs, out_specs=out_specs, check_vma=False
    )
```

```python
import functools

import jax
import jax.numpy as jnp
from jax import lax
from jax.experimental import pallas as pl
from jax.experimental.pallas import tpu as pltpu
from jax.sharding import PartitionSpec as P

MESH = pl.DeviceIdType.MESH
CAP = 5
EPSILON = 1e-06
FIELDS = 9
BLOCK = 16
SENT = 12
F32 = jnp.float32
BF16 = jnp.bfloat16
HIGHEST = lax.Precision.HIGHEST


def iota(shape, dim):
    return lax.broadcasted_iota(jnp.int32, shape, dim)


def dot(a, b):
    return jnp.dot(a, b, preferred_element_type=F32)


def dot_back(a, b):
    return lax.dot_general(a, b, (((1,), (1,)), ((), ())), preferred_element_type=F32)


def dot_rows(a, b):
    return lax.dot_general(a, b, (((0,), (0,)), ((), ())), preferred_element_type=F32)


def slot_of_lane(lane):
    return lax.shift_right_logical(lane * 57, 9)


def farthest_first(tile, tiles, ring, send):
    outer = tiles // ring
    line, place = tile // ring, lax.rem(tile, ring)

    def one(turn, across):
        step = (turn + 1) // 2
        along = jnp.where(lax.rem(turn, 2) == 1, ring // 2 + step, ring // 2 - step)
        send(lax.rem(line + across, outer) * ring + lax.rem(place + along, ring))

    @pl.loop(0, ring - 1)
    def _(turn):
        for across in range(outer):
            one(turn, (across + outer // 2) % outer)

    for across in range(1, outer):
        send(lax.rem(line + across, outer) * ring + place)


def pack_reports(steps, tiles, owner_ref, stencil_ref, weights_ref, values_ref, precision_ref, mt):
    rows = values_ref.shape[1]
    lane = iota((rows, 128), 1)
    row = iota((rows, 128), 0)
    lane_slot = slot_of_lane(lane)
    lane_field = lane - FIELDS * lane_slot
    spread_fields = jnp.where((row == lane_field) & (row < FIELDS), 1.0, 0.0).astype(BF16)
    place = iota((tiles * BLOCK, rows), 0)
    one_hots, operands = [], []
    mt[...] = jnp.zeros_like(mt)
    for k in range(steps):
        owner_row = owner_ref[k]
        mt[k, 0:4, :] = stencil_ref[k].astype(F32)
        mt[k, 4:8, :] = weights_ref[k].astype(F32)
        mt[k, 8:9, :] = precision_ref[0, k : k + 1, :].astype(F32)
        mt[k, 9:10, :] = owner_row.astype(F32)
        columns = mt[k].T
        owner_col = columns[:, 9:10].astype(jnp.int32)
        same = owner_col == owner_row
        rank_row = jnp.sum(jnp.where(same & (row < lane), 1, 0), axis=0, keepdims=True)
        rank_col = jnp.sum(jnp.where(same & (lane < row), 1, 0), axis=1, keepdims=True)
        meta = dot(columns.astype(BF16), spread_fields)
        meta = jnp.where(lane_slot == rank_col + CAP * k, meta, 0.0).astype(BF16)
        base = owner_row * BLOCK
        one_hots.append(jnp.where(place == base + (rank_row + CAP * k), 1.0, 0.0).astype(BF16))
        operands.append(values_ref[k])
        one_hots.append(jnp.where(place == base + CAP * steps, 1.0, 0.0).astype(BF16))
        operands.append(meta)
    return dot(jnp.concatenate(one_hots, axis=1), jnp.concatenate(operands, axis=0)).astype(BF16)


def report_operators(steps, tiles, arrived, cells):
    slots = CAP * steps
    meta = arrived[:, slots, :]
    lane_slot = slot_of_lane(iota((tiles, 128), 1))
    stacked = jnp.concatenate(
        [jnp.where(lane_slot == s, meta, 0.0) for s in range(slots)], axis=0
    ).astype(BF16)
    values = jnp.concatenate([arrived[:, s, :] for s in range(slots)], axis=0)
    lane = iota((128, 384), 0)
    column = iota((128, 384), 1)
    field = lane - FIELDS * slot_of_lane(lane)
    wanted = jnp.minimum(lax.shift_right_logical(column, 5), FIELDS - 1)
    expand = jnp.where((field == wanted) & (lane < FIELDS * slots), 1.0, 0.0).astype(BF16)
    expanded = dot(stacked, expand)
    cell = jnp.bitwise_and(iota((tiles * slots, 128), 1), cells - 1).astype(F32)
    table = jnp.where(expanded[:, 0:128] == cell, expanded[:, 128:256], 0.0)
    precision = expanded[:, 256:384]
    right = jnp.concatenate([precision * table, precision * values], axis=1)
    table = table.astype(BF16)
    high = right.astype(BF16)
    low = (right - high.astype(F32)).astype(BF16)
    r = iota((128, 128), 0)
    c = iota((128, 128), 1)
    fold = jnp.where(jnp.bitwise_and(r, cells - 1) == jnp.bitwise_and(c, cells - 1), 1.0, 0.0)
    member = lax.shift_right_logical(r, 5) == lax.shift_right_logical(c, 5)
    out = []
    for k in range(steps):
        part = slice(k * CAP * tiles, (k + 1) * CAP * tiles)
        both = dot_rows(table[part], high[part]) + dot_rows(table[part], low[part])
        both = jnp.dot(fold, both, precision=HIGHEST, preferred_element_type=F32)
        gram = jnp.dot(both[:, 0:128], fold, precision=HIGHEST, preferred_element_type=F32)
        out.append((jnp.where(member, gram, 0.0), both[:, 128:256]))
    return out


def kernel(
    slots,
    tiles,
    ring,
    steps,
    control_hbm,
    background_hbm,
    self_hbm,
    neighbour_hbm,
    output_hbm,
    gain_hbm,
    readout_hbm,
    error_hbm,
    owner_hbm,
    stencil_hbm,
    weights_hbm,
    values_hbm,
    precision_hbm,
    out_ref,
    control_ref,
    background_ref,
    self_ref,
    neighbour_ref,
    output_ref,
    gain_ref,
    readout_ref,
    error_ref,
    owner_ref,
    stencil_ref,
    weights_ref,
    values_ref,
    precision_ref,
    fetch_sem,
    mt,
    send_buf,
    recv_buf,
    arrived,
    edge_send,
    edge_recv,
    own,
    west,
    east,
    next_control,
    final_send,
    final_recv,
    report_send_sem,
    report_recv_sem,
    edge_send_sem,
    edge_recv_sem,
    state_send_sem,
    state_recv_sem,
    wide_send,
    wide_recv,
    spread_send,
    spread_recv,
    wide_spread,
    side_send_sem,
    side_recv_sem,
):
    slot = lax.axis_index("slot")
    tile = lax.axis_index("tile")
    east_tile, west_tile = lax.rem(tile + 1, tiles), lax.rem(tile + tiles - 1, tiles)
    next_slot, last_slot = lax.rem(slot + 1, slots), lax.rem(slot + slots - 1, slots)
    rows, channels = control_ref.shape
    groups = rows // BLOCK

    fetches = [
        pltpu.make_async_copy(source, target, fetch_sem.at[i])
        for i, (source, target) in enumerate(
            (
                (control_hbm, control_ref),
                (gain_hbm, gain_ref),
                (owner_hbm, owner_ref),
                (stencil_hbm, stencil_ref),
                (weights_hbm, weights_ref),
                (precision_hbm, precision_ref),
                (values_hbm, values_ref),
                (self_hbm, self_ref),
                (neighbour_hbm, neighbour_ref),
                (output_hbm, output_ref),
                (readout_hbm, readout_ref),
                (error_hbm, error_ref),
                (background_hbm, background_ref),
            )
        )
    ]
    barrier = pltpu.get_barrier_semaphore()

    def greet(peer):
        pl.semaphore_signal(barrier, inc=1, device_id=(slot, peer), device_id_type=MESH)

    farthest_first(tile, tiles, ring, greet)
    for peer in (next_slot, last_slot):
        pl.semaphore_signal(barrier, inc=1, device_id=(peer, tile), device_id_type=MESH)

    for fetch in fetches:
        fetch.start()

    def edge_copy(turn, side):
        return pltpu.make_async_remote_copy(
            src_ref=edge_send.at[turn, side],
            dst_ref=edge_recv.at[turn, side],
            send_sem=edge_send_sem.at[turn, side],
            recv_sem=edge_recv_sem.at[turn, side],
            device_id=(slot, east_tile if side == 0 else west_tile),
            device_id_type=MESH,
        )

    def set_edges(turn, rounded):
        own[...] = rounded.astype(F32).reshape(groups, BLOCK, channels)
        edge_send[turn, 0] = own[:, BLOCK - 1, :].astype(BF16)
        edge_send[turn, 1] = own[:, 0, :].astype(BF16)

    def send_edges(turn):
        edge_copy(turn, 0).start()
        edge_copy(turn, 1).start()

    def shift_rows():
        whole = own[...].reshape(rows, channels)
        west[...] = pltpu.roll(whole, 1, 0).reshape(groups, BLOCK, channels)
        east[...] = pltpu.roll(whole, rows - 1, 0).reshape(groups, BLOCK, channels)

    def neighbours(turn=None, halo=None):
        whole = own[...].reshape(rows, channels)
        swapped = jnp.concatenate(
            [whole[BLOCK * (g ^ 1) : BLOCK * (g ^ 1) + BLOCK] for g in range(groups)], axis=0
        )
        if halo is None:
            edge_copy(turn, 0).wait_recv()
            edge_copy(turn, 1).wait_recv()
            halo = edge_recv[turn, 0].astype(F32), edge_recv[turn, 1].astype(F32)
        west[:, 0, :], east[:, BLOCK - 1, :] = halo
        return (
            swapped
            + west[...].reshape(rows, channels)
            + east[...].reshape(rows, channels)
        )

    for fetch in fetches:
        fetch.wait()
    def side_copy(source, target, index, side):
        return pltpu.make_async_remote_copy(
            src_ref=source.at[side],
            dst_ref=target.at[side],
            send_sem=side_send_sem.at[index, side],
            recv_sem=side_recv_sem.at[index, side],
            device_id=(slot, east_tile if side == 0 else west_tile),
            device_id_type=MESH,
        )

    side_copies = [
        side_copy(source, target, index, side)
        for index, (source, target) in enumerate(
            ((wide_send, wide_recv), (spread_send, spread_recv))
        )
        for side in range(2)
    ]

    def border(scratch, value, depth):
        scratch[...] = value.reshape(scratch.shape)
        return [
            [scratch[:, BLOCK - 1 - d, :] for d in range(depth)],
            [scratch[:, d, :] for d in range(depth)],
        ]

    def send_borders(buffer, first_copy, parts):
        for side in range(2):
            flat = [piece for part in parts for piece in part[side]]
            buffer[side] = jnp.concatenate(flat, axis=0).astype(BF16)
            side_copies[first_copy + side].start()

    gain = gain_ref[...]

    def normalize(current):
        inverse_rms = lax.rsqrt(jnp.mean(current * current, axis=-1, keepdims=True) + EPSILON)
        return (current * inverse_rms * gain).astype(BF16), inverse_rms

    control_copy = pltpu.make_async_remote_copy(
        src_ref=control_ref,
        dst_ref=next_control,
        send_sem=state_send_sem.at[0],
        recv_sem=state_recv_sem.at[0],
        device_id=(last_slot, tile),
        device_id_type=MESH,
    )
    final_copy = pltpu.make_async_remote_copy(
        src_ref=final_send,
        dst_ref=final_recv,
        send_sem=state_send_sem.at[1],
        recv_sem=state_recv_sem.at[1],
        device_id=(next_slot, tile),
        device_id_type=MESH,
    )

    current = control_ref[...]
    normed, inverse_rms = normalize(current)
    set_edges(0, normed)
    packed = pack_reports(
        steps, tiles, owner_ref, stencil_ref, weights_ref, values_ref, precision_ref, mt
    )
    send_buf[...] = packed.reshape(tiles, BLOCK, 128)
    pl.semaphore_wait(barrier, tiles + 1)
    send_edges(0)

    def send_reports(peer):
        pltpu.make_async_remote_copy(
            src_ref=send_buf.at[peer, 0:SENT],
            dst_ref=recv_buf.at[tile, 0:SENT],
            send_sem=report_send_sem,
            recv_sem=report_recv_sem,
            device_id=(slot, peer),
            device_id_type=MESH,
        ).start()

    farthest_first(tile, tiles, ring, send_reports)
    control_copy.start()
    recv_buf[pl.ds(tile, 1)] = send_buf[pl.ds(tile, 1)]

    states, kept, fields = [], [], []
    for k in range(steps):
        if k > 0:
            normed, inverse_rms = normalize(current)
            set_edges(k, normed)
            send_edges(k)
        linear = dot(normed, self_ref[...])
        shift_rows()
        mixed = (0.25 * neighbours(k)).astype(BF16)
        linear = linear + dot(mixed, neighbour_ref[...])
        sigmoid = 1.0 / (1.0 + jnp.exp(-linear))
        states.append(current)
        kept.append((inverse_rms, sigmoid * (1.0 + linear * (1.0 - sigmoid))))
        current = current + dot((linear * sigmoid).astype(BF16), output_ref[...])
        fields.append(dot(current.astype(BF16), readout_ref[...]))
    final = current.astype(BF16)
    final_send[...] = final
    final_copy.start()

    error = error_ref[...]
    control_copy.wait_recv()
    next_misfit = error * (next_control[...] - final.astype(F32))
    next_misfit = jnp.where(slot == slots - 1, 0.0, next_misfit)
    send_borders(
        wide_send,
        0,
        [
            border(own, kept[1][1], 2),
            border(west, next_misfit, 2),
            border(east, kept[0][1], 1),
            border(own, states[1], 1),
        ],
    )

    others = pl.ds(0, tiles - 1)
    everyone = pltpu.make_async_remote_copy(
        src_ref=send_buf.at[others, 0:SENT],
        dst_ref=recv_buf.at[others, 0:SENT],
        send_sem=report_send_sem,
        recv_sem=report_recv_sem,
        device_id=(slot, east_tile),
        device_id_type=MESH,
    )
    everyone.wait_recv()
    arrived[...] = recv_buf[...].astype(F32)
    spreads, pulls = [], []
    for (gram, offset), field in zip(report_operators(steps, tiles, arrived, 2 * BLOCK), fields):
        spread = jnp.dot(gram, field, precision=HIGHEST, preferred_element_type=F32) - offset
        spreads.append(spread.astype(BF16))
    send_borders(
        spread_send,
        2,
        [
            border(wide_spread, spreads[1].astype(F32), 2),
            border(wide_spread, spreads[0].astype(F32), 1),
        ],
    )
    for spread in spreads:
        pulls.append(dot_back(spread, readout_ref[...]))
    cotangent = pulls[1] - next_misfit

    def beyond(buffer, index):
        piece = slice(groups * index, groups * (index + 1))
        return [buffer[side].astype(F32)[piece] for side in range(2)]

    side_copies[0].wait_recv()
    side_copies[1].wait_recv()
    wide_slope = jnp.concatenate(beyond(wide_recv, 0) + beyond(wide_recv, 1), axis=0)
    wide_misfit = jnp.concatenate(beyond(wide_recv, 2) + beyond(wide_recv, 3), axis=0)
    wide_slope_0 = jnp.concatenate(beyond(wide_recv, 4), axis=0)
    wide_state = jnp.concatenate(beyond(wide_recv, 5), axis=0)
    side_copies[2].wait_recv()
    side_copies[3].wait_recv()
    wide_pull = dot_back(
        jnp.concatenate(
            beyond(spread_recv, 0) + beyond(spread_recv, 1) + beyond(spread_recv, 2), axis=0
        ).astype(BF16),
        readout_ref[...],
    )
    close = 2 * groups
    wide = wide_pull[0 : 2 * close] - wide_misfit

    def pulled_back(inner, outer, inner_slope, outer_slope):
        both = jnp.concatenate([inner, outer], axis=0).astype(BF16)
        slope = jnp.concatenate([inner_slope, outer_slope], axis=0)
        back = (dot_back(both, output_ref[...]) * slope).astype(BF16)
        mixed = dot_back(back, neighbour_ref[...]).astype(BF16).astype(F32)
        own[...] = mixed[0:rows].reshape(groups, BLOCK, channels)
        shift_rows()
        return dot_back(back, self_ref[...]), mixed[rows:]

    def adjoint(state, inverse_rms, cotangent, grad_normed):
        scaled = gain * grad_normed
        mean = jnp.mean(state * scaled, axis=-1, keepdims=True)
        cubed = inverse_rms * inverse_rms * inverse_rms
        return cotangent + inverse_rms * scaled - state * (cubed * mean)

    direct, mixed = pulled_back(cotangent, wide, kept[1][1], wide_slope)
    halo = mixed[0:groups], mixed[groups:close]
    even = lax.rem(iota((close, channels), 0), 2) == 0
    beside = jnp.where(
        even, pltpu.roll(mixed[0:close], close - 1, 0), pltpu.roll(mixed[0:close], 1, 0)
    )
    beside = beside + mixed[close:]
    beside = beside + jnp.concatenate([own[:, 0, :], own[:, BLOCK - 1, :]], axis=0)
    wide = adjoint(
        wide_state,
        lax.rsqrt(jnp.mean(wide_state * wide_state, axis=-1, keepdims=True) + EPSILON),
        wide[0:close],
        direct[rows : rows + close] + 0.25 * beside,
    )
    wide = wide + wide_pull[2 * close :]
    cotangent = adjoint(
        states[1], kept[1][0], cotangent, direct[0:rows] + 0.25 * neighbours(halo=halo)
    )
    cotangent = cotangent + pulls[0]

    direct, mixed = pulled_back(cotangent, wide, kept[0][1], wide_slope_0)
    halo = mixed[0:groups], mixed[groups:close]
    cotangent = adjoint(
        states[0], kept[0][0], cotangent, direct[0:rows] + 0.25 * neighbours(halo=halo)
    )

    final_copy.wait_recv()
    previous = jnp.where(slot == 0, background_ref[...].astype(F32), final_recv[...].astype(F32))
    out_ref[...] = cotangent + error * (control_ref[...] - previous)

    everyone.wait_send()
    for copy in side_copies:
        copy.wait_send()
    for turn in range(steps):
        edge_copy(turn, 0).wait_send()
        edge_copy(turn, 1).wait_send()
    control_copy.wait_send()
    final_copy.wait_send()


def solution(mesh):
    slots, tiles = mesh.shape["slot"], mesh.shape["tile"]

    def per_device(
        control,
        background,
        self_weight,
        neighbour_weight,
        output_weight,
        norm_gain,
        readout,
        error_weight,
        report_owner,
        report_stencil,
        report_weights,
        report_values,
        report_precision,
    ):
        channels = control.shape[-1]
        rows = control.size // channels
        steps = report_values.shape[1]
        groups = rows // BLOCK
        ring = 16 if tiles % 16 == 0 else tiles
        edges = (steps, 2, groups, channels)
        block = (groups, BLOCK, channels)
        message = (tiles, BLOCK, 128)
        operands = (
            control.reshape(rows, channels),
            background.reshape(rows, channels),
            self_weight,
            neighbour_weight,
            output_weight,
            norm_gain.reshape(1, channels),
            readout,
            error_weight.reshape(1, channels),
            report_owner[0].transpose(0, 2, 1),
            report_stencil[0].transpose(0, 2, 1),
            report_weights[0].transpose(0, 2, 1),
            report_values[0],
            report_precision,
        )
        out = pl.pallas_call(
            functools.partial(kernel, slots, tiles, ring, steps),
            out_shape=jax.ShapeDtypeStruct((rows, channels), F32),
            in_specs=[pl.BlockSpec(memory_space=pl.ANY)] * len(operands),
            out_specs=pl.BlockSpec(memory_space=pltpu.VMEM),
            scratch_shapes=[
                *[pltpu.VMEM(operand.shape, operand.dtype) for operand in operands],
                pltpu.SemaphoreType.DMA((len(operands),)),
                pltpu.VMEM((steps, 128, 128), F32),
                pltpu.VMEM(message, BF16),
                pltpu.VMEM(message, BF16),
                pltpu.VMEM(message, F32),
                pltpu.VMEM(edges, BF16),
                pltpu.VMEM(edges, BF16),
                pltpu.VMEM(block, F32),
                pltpu.VMEM(block, F32),
                pltpu.VMEM(block, F32),
                pltpu.VMEM((rows, channels), F32),
                pltpu.VMEM((rows, channels), BF16),
                pltpu.VMEM((rows, channels), BF16),
                pltpu.SemaphoreType.DMA,
                pltpu.SemaphoreType.DMA,
                pltpu.SemaphoreType.DMA((steps, 2)),
                pltpu.SemaphoreType.DMA((steps, 2)),
                pltpu.SemaphoreType.DMA((2,)),
                pltpu.SemaphoreType.DMA((2,)),
                pltpu.VMEM((2, 6 * groups, channels), BF16),
                pltpu.VMEM((2, 6 * groups, channels), BF16),
                pltpu.VMEM((2, 3 * groups, 128), BF16),
                pltpu.VMEM((2, 3 * groups, 128), BF16),
                pltpu.VMEM((groups, BLOCK, 128), F32),
                pltpu.SemaphoreType.DMA((2, 2)),
                pltpu.SemaphoreType.DMA((2, 2)),
            ],
            compiler_params=pltpu.CompilerParams(collective_id=0, has_side_effects=True),
        )(*operands)
        return out.reshape(control.shape)

    in_specs = (
        P("slot", None, None, "tile", None),
        P(None, None, "tile", None),
        P(),
        P(),
        P(),
        P(),
        P(),
        P(),
        P("slot", None, "tile", None),
        P("slot", None, "tile", None),
        P("slot", None, "tile", None),
        P("slot", None, "tile", None),
        P("slot", None, "tile"),
    )
    out_specs = P("slot", None, None, "tile", None)
    return jax.shard_map(
        per_device, mesh=mesh, in_specs=in_specs, out_specs=out_specs, check_vma=False
    )
```

```python
import functools

import jax
import jax.numpy as jnp
from jax import lax
from jax.experimental import pallas as pl
from jax.experimental.pallas import tpu as pltpu
from jax.sharding import PartitionSpec as P

MESH = pl.DeviceIdType.MESH
CAP = 5
EPSILON = 1e-06
FIELDS = 9
BLOCK = 16
SENT = 12
F32 = jnp.float32
BF16 = jnp.bfloat16
HIGHEST = lax.Precision.HIGHEST


def iota(shape, dim):
    return lax.broadcasted_iota(jnp.int32, shape, dim)


def dot(a, b):
    return jnp.dot(a, b, preferred_element_type=F32)


def dot_back(a, b):
    return lax.dot_general(a, b, (((1,), (1,)), ((), ())), preferred_element_type=F32)


def dot_rows(a, b):
    return lax.dot_general(a, b, (((0,), (0,)), ((), ())), preferred_element_type=F32)


def slot_of_lane(lane):
    return lax.shift_right_logical(lane * 57, 9)


def farthest_first(tile, tiles, ring, send):
    outer = tiles // ring
    line, place = tile // ring, lax.rem(tile, ring)

    def one(turn, across):
        step = (turn + 1) // 2
        along = jnp.where(lax.rem(turn, 2) == 1, ring // 2 + step, ring // 2 - step)
        send(lax.rem(line + across, outer) * ring + lax.rem(place + along, ring))

    @pl.loop(0, ring - 1)
    def _(turn):
        for across in range(outer):
            one(turn, (across + outer // 2) % outer)

    for across in range(1, outer):
        send(lax.rem(line + across, outer) * ring + place)


def pack_reports(steps, tiles, owner_ref, stencil_ref, weights_ref, values_ref, precision_ref, mt):
    rows = values_ref.shape[1]
    lane = iota((rows, 128), 1)
    row = iota((rows, 128), 0)
    lane_slot = slot_of_lane(lane)
    lane_field = lane - FIELDS * lane_slot
    spread_fields = jnp.where((row == lane_field) & (row < FIELDS), 1.0, 0.0).astype(BF16)
    place = iota((tiles * BLOCK, rows), 0)
    one_hots, operands = [], []
    mt[...] = jnp.zeros_like(mt)
    for k in range(steps):
        owner_row = owner_ref[k]
        mt[k, 0:4, :] = stencil_ref[k].astype(F32)
        mt[k, 4:8, :] = weights_ref[k].astype(F32)
        mt[k, 8:9, :] = precision_ref[0, k : k + 1, :].astype(F32)
        mt[k, 9:10, :] = owner_row.astype(F32)
        columns = mt[k].T
        owner_col = columns[:, 9:10].astype(jnp.int32)
        same = owner_col == owner_row
        rank_row = jnp.sum(jnp.where(same & (row < lane), 1, 0), axis=0, keepdims=True)
        rank_col = jnp.sum(jnp.where(same & (lane < row), 1, 0), axis=1, keepdims=True)
        meta = dot(columns.astype(BF16), spread_fields)
        meta = jnp.where(lane_slot == rank_col + CAP * k, meta, 0.0).astype(BF16)
        base = owner_row * BLOCK
        one_hots.append(jnp.where(place == base + (rank_row + CAP * k), 1.0, 0.0).astype(BF16))
        operands.append(values_ref[k])
        one_hots.append(jnp.where(place == base + CAP * steps, 1.0, 0.0).astype(BF16))
        operands.append(meta)
    return dot(jnp.concatenate(one_hots, axis=1), jnp.concatenate(operands, axis=0)).astype(BF16)


def report_operators(steps, tiles, arrived, cells):
    slots = CAP * steps
    meta = arrived[:, slots, :]
    lane_slot = slot_of_lane(iota((tiles, 128), 1))
    stacked = jnp.concatenate(
        [jnp.where(lane_slot == s, meta, 0.0) for s in range(slots)], axis=0
    ).astype(BF16)
    values = jnp.concatenate([arrived[:, s, :] for s in range(slots)], axis=0)
    lane = iota((128, 384), 0)
    column = iota((128, 384), 1)
    field = lane - FIELDS * slot_of_lane(lane)
    wanted = jnp.minimum(lax.shift_right_logical(column, 5), FIELDS - 1)
    expand = jnp.where((field == wanted) & (lane < FIELDS * slots), 1.0, 0.0).astype(BF16)
    expanded = dot(stacked, expand)
    cell = jnp.bitwise_and(iota((tiles * slots, 128), 1), cells - 1).astype(F32)
    table = jnp.where(expanded[:, 0:128] == cell, expanded[:, 128:256], 0.0)
    precision = expanded[:, 256:384]
    right = jnp.concatenate([precision * table, precision * values], axis=1)
    table = table.astype(BF16)
    high = right.astype(BF16)
    low = (right - high.astype(F32)).astype(BF16)
    r = iota((128, 128), 0)
    c = iota((128, 128), 1)
    fold = jnp.where(jnp.bitwise_and(r, cells - 1) == jnp.bitwise_and(c, cells - 1), 1.0, 0.0)
    member = lax.shift_right_logical(r, 5) == lax.shift_right_logical(c, 5)
    out = []
    for k in range(steps):
        part = slice(k * CAP * tiles, (k + 1) * CAP * tiles)
        both = dot_rows(table[part], high[part]) + dot_rows(table[part], low[part])
        both = jnp.dot(fold, both, precision=HIGHEST, preferred_element_type=F32)
        gram = jnp.dot(both[:, 0:128], fold, precision=HIGHEST, preferred_element_type=F32)
        out.append((jnp.where(member, gram, 0.0), both[:, 128:256]))
    return out


def kernel(
    slots,
    tiles,
    ring,
    steps,
    control_hbm,
    background_hbm,
    self_hbm,
    neighbour_hbm,
    output_hbm,
    gain_hbm,
    readout_hbm,
    error_hbm,
    owner_hbm,
    stencil_hbm,
    weights_hbm,
    values_hbm,
    precision_hbm,
    out_ref,
    control_ref,
    background_ref,
    self_ref,
    neighbour_ref,
    output_ref,
    gain_ref,
    readout_ref,
    error_ref,
    owner_ref,
    stencil_ref,
    weights_ref,
    values_ref,
    precision_ref,
    fetch_sem,
    mt,
    send_buf,
    recv_buf,
    arrived,
    edge_send,
    edge_recv,
    own,
    west,
    east,
    next_control,
    final_send,
    final_recv,
    report_send_sem,
    report_recv_sem,
    edge_send_sem,
    edge_recv_sem,
    state_send_sem,
    state_recv_sem,
    wide_send,
    wide_recv,
    late_send,
    late_recv,
    spread_send,
    spread_recv,
    wide_spread,
    side_send_sem,
    side_recv_sem,
):
    slot = lax.axis_index("slot")
    tile = lax.axis_index("tile")
    east_tile, west_tile = lax.rem(tile + 1, tiles), lax.rem(tile + tiles - 1, tiles)
    next_slot, last_slot = lax.rem(slot + 1, slots), lax.rem(slot + slots - 1, slots)
    rows, channels = control_ref.shape
    groups = rows // BLOCK

    fetches = [
        pltpu.make_async_copy(source, target, fetch_sem.at[i])
        for i, (source, target) in enumerate(
            (
                (control_hbm, control_ref),
                (gain_hbm, gain_ref),
                (owner_hbm, owner_ref),
                (stencil_hbm, stencil_ref),
                (weights_hbm, weights_ref),
                (precision_hbm, precision_ref),
                (values_hbm, values_ref),
                (self_hbm, self_ref),
                (neighbour_hbm, neighbour_ref),
                (output_hbm, output_ref),
                (readout_hbm, readout_ref),
                (error_hbm, error_ref),
                (background_hbm, background_ref),
            )
        )
    ]
    barrier = pltpu.get_barrier_semaphore()

    def greet(peer):
        pl.semaphore_signal(barrier, inc=1, device_id=(slot, peer), device_id_type=MESH)

    farthest_first(tile, tiles, ring, greet)
    for peer in (next_slot, last_slot):
        pl.semaphore_signal(barrier, inc=1, device_id=(peer, tile), device_id_type=MESH)

    for fetch in fetches:
        fetch.start()

    def edge_copy(turn, side):
        return pltpu.make_async_remote_copy(
            src_ref=edge_send.at[turn, side],
            dst_ref=edge_recv.at[turn, side],
            send_sem=edge_send_sem.at[turn, side],
            recv_sem=edge_recv_sem.at[turn, side],
            device_id=(slot, east_tile if side == 0 else west_tile),
            device_id_type=MESH,
        )

    def set_edges(turn, rounded):
        own[...] = rounded.astype(F32).reshape(groups, BLOCK, channels)
        edge_send[turn, 0] = own[:, BLOCK - 1, :].astype(BF16)
        edge_send[turn, 1] = own[:, 0, :].astype(BF16)

    def send_edges(turn):
        edge_copy(turn, 0).start()
        edge_copy(turn, 1).start()

    def shift_rows():
        whole = own[...].reshape(rows, channels)
        west[...] = pltpu.roll(whole, 1, 0).reshape(groups, BLOCK, channels)
        east[...] = pltpu.roll(whole, rows - 1, 0).reshape(groups, BLOCK, channels)

    def neighbours(turn=None, halo=None):
        whole = own[...].reshape(rows, channels)
        swapped = jnp.concatenate(
            [whole[BLOCK * (g ^ 1) : BLOCK * (g ^ 1) + BLOCK] for g in range(groups)], axis=0
        )
        if halo is None:
            edge_copy(turn, 0).wait_recv()
            edge_copy(turn, 1).wait_recv()
            halo = edge_recv[turn, 0].astype(F32), edge_recv[turn, 1].astype(F32)
        west[:, 0, :], east[:, BLOCK - 1, :] = halo
        return (
            swapped
            + west[...].reshape(rows, channels)
            + east[...].reshape(rows, channels)
        )

    for fetch in fetches:
        fetch.wait()
    def side_copy(source, target, index, side):
        return pltpu.make_async_remote_copy(
            src_ref=source.at[side],
            dst_ref=target.at[side],
            send_sem=side_send_sem.at[index, side],
            recv_sem=side_recv_sem.at[index, side],
            device_id=(slot, east_tile if side == 0 else west_tile),
            device_id_type=MESH,
        )

    side_copies = [
        side_copy(source, target, index, side)
        for index, (source, target) in enumerate(
            ((wide_send, wide_recv), (spread_send, spread_recv), (late_send, late_recv))
        )
        for side in range(2)
    ]

    def border(scratch, value, depth):
        scratch[...] = value.reshape(scratch.shape)
        return [
            [scratch[:, BLOCK - 1 - d, :] for d in range(depth)],
            [scratch[:, d, :] for d in range(depth)],
        ]

    def send_borders(buffer, first_copy, parts):
        for side in range(2):
            flat = [piece for part in parts for piece in part[side]]
            buffer[side] = jnp.concatenate(flat, axis=0).astype(BF16)
            side_copies[first_copy + side].start()

    gain = gain_ref[...]

    def normalize(current):
        inverse_rms = lax.rsqrt(jnp.mean(current * current, axis=-1, keepdims=True) + EPSILON)
        return (current * inverse_rms * gain).astype(BF16), inverse_rms

    control_copy = pltpu.make_async_remote_copy(
        src_ref=control_ref,
        dst_ref=next_control,
        send_sem=state_send_sem.at[0],
        recv_sem=state_recv_sem.at[0],
        device_id=(last_slot, tile),
        device_id_type=MESH,
    )
    final_copy = pltpu.make_async_remote_copy(
        src_ref=final_send,
        dst_ref=final_recv,
        send_sem=state_send_sem.at[1],
        recv_sem=state_recv_sem.at[1],
        device_id=(next_slot, tile),
        device_id_type=MESH,
    )

    current = control_ref[...]
    normed, inverse_rms = normalize(current)
    set_edges(0, normed)
    packed = pack_reports(
        steps, tiles, owner_ref, stencil_ref, weights_ref, values_ref, precision_ref, mt
    )
    send_buf[...] = packed.reshape(tiles, BLOCK, 128)
    pl.semaphore_wait(barrier, tiles + 1)
    send_edges(0)

    def send_reports(peer):
        pltpu.make_async_remote_copy(
            src_ref=send_buf.at[peer, 0:SENT],
            dst_ref=recv_buf.at[tile, 0:SENT],
            send_sem=report_send_sem,
            recv_sem=report_recv_sem,
            device_id=(slot, peer),
            device_id_type=MESH,
        ).start()

    farthest_first(tile, tiles, ring, send_reports)
    control_copy.start()
    recv_buf[pl.ds(tile, 1)] = send_buf[pl.ds(tile, 1)]

    states, kept, fields = [], [], []
    for k in range(steps):
        if k > 0:
            normed, inverse_rms = normalize(current)
            set_edges(k, normed)
            send_edges(k)
        linear = dot(normed, self_ref[...])
        shift_rows()
        mixed = (0.25 * neighbours(k)).astype(BF16)
        linear = linear + dot(mixed, neighbour_ref[...])
        sigmoid = 1.0 / (1.0 + jnp.exp(-linear))
        states.append(current)
        kept.append((inverse_rms, sigmoid * (1.0 + linear * (1.0 - sigmoid))))
        if k == 1:
            send_borders(
                wide_send,
                0,
                [
                    border(own, kept[1][1], 2),
                    border(east, kept[0][1], 1),
                    border(own, states[1], 1),
                ],
            )
        current = current + dot((linear * sigmoid).astype(BF16), output_ref[...])
        fields.append(dot(current.astype(BF16), readout_ref[...]))
    final = current.astype(BF16)
    final_send[...] = final
    final_copy.start()

    error = error_ref[...]
    control_copy.wait_recv()
    next_misfit = error * (next_control[...] - final.astype(F32))
    next_misfit = jnp.where(slot == slots - 1, 0.0, next_misfit)
    send_borders(late_send, 4, [border(west, next_misfit, 2)])

    others = pl.ds(0, tiles - 1)
    everyone = pltpu.make_async_remote_copy(
        src_ref=send_buf.at[others, 0:SENT],
        dst_ref=recv_buf.at[others, 0:SENT],
        send_sem=report_send_sem,
        recv_sem=report_recv_sem,
        device_id=(slot, east_tile),
        device_id_type=MESH,
    )
    everyone.wait_recv()
    arrived[...] = recv_buf[...].astype(F32)
    spreads, pulls = [], []
    for (gram, offset), field in zip(report_operators(steps, tiles, arrived, 2 * BLOCK), fields):
        spread = jnp.dot(gram, field, precision=HIGHEST, preferred_element_type=F32) - offset
        spreads.append(spread.astype(BF16))
    send_borders(
        spread_send,
        2,
        [
            border(wide_spread, spreads[1].astype(F32), 2),
            border(wide_spread, spreads[0].astype(F32), 1),
        ],
    )
    for spread in spreads:
        pulls.append(dot_back(spread, readout_ref[...]))
    cotangent = pulls[1] - next_misfit

    def beyond(buffer, index):
        piece = slice(groups * index, groups * (index + 1))
        return [buffer[side].astype(F32)[piece] for side in range(2)]

    side_copies[0].wait_recv()
    side_copies[1].wait_recv()
    side_copies[4].wait_recv()
    side_copies[5].wait_recv()
    wide_slope = jnp.concatenate(beyond(wide_recv, 0) + beyond(wide_recv, 1), axis=0)
    wide_misfit = jnp.concatenate(beyond(late_recv, 0) + beyond(late_recv, 1), axis=0)
    wide_slope_0 = jnp.concatenate(beyond(wide_recv, 2), axis=0)
    wide_state = jnp.concatenate(beyond(wide_recv, 3), axis=0)
    side_copies[2].wait_recv()
    side_copies[3].wait_recv()
    wide_pull = dot_back(
        jnp.concatenate(
            beyond(spread_recv, 0) + beyond(spread_recv, 1) + beyond(spread_recv, 2), axis=0
        ).astype(BF16),
        readout_ref[...],
    )
    close = 2 * groups
    wide = wide_pull[0 : 2 * close] - wide_misfit

    def pulled_back(inner, outer, inner_slope, outer_slope):
        both = jnp.concatenate([inner, outer], axis=0).astype(BF16)
        slope = jnp.concatenate([inner_slope, outer_slope], axis=0)
        back = (dot_back(both, output_ref[...]) * slope).astype(BF16)
        mixed = dot_back(back, neighbour_ref[...]).astype(BF16).astype(F32)
        own[...] = mixed[0:rows].reshape(groups, BLOCK, channels)
        shift_rows()
        return dot_back(back, self_ref[...]), mixed[rows:]

    def adjoint(state, inverse_rms, cotangent, grad_normed):
        scaled = gain * grad_normed
        mean = jnp.mean(state * scaled, axis=-1, keepdims=True)
        cubed = inverse_rms * inverse_rms * inverse_rms
        return cotangent + inverse_rms * scaled - state * (cubed * mean)

    direct, mixed = pulled_back(cotangent, wide, kept[1][1], wide_slope)
    halo = mixed[0:groups], mixed[groups:close]
    even = lax.rem(iota((close, channels), 0), 2) == 0
    beside = jnp.where(
        even, pltpu.roll(mixed[0:close], close - 1, 0), pltpu.roll(mixed[0:close], 1, 0)
    )
    beside = beside + mixed[close:]
    beside = beside + jnp.concatenate([own[:, 0, :], own[:, BLOCK - 1, :]], axis=0)
    wide = adjoint(
        wide_state,
        lax.rsqrt(jnp.mean(wide_state * wide_state, axis=-1, keepdims=True) + EPSILON),
        wide[0:close],
        direct[rows : rows + close] + 0.25 * beside,
    )
    wide = wide + wide_pull[2 * close :]
    cotangent = adjoint(
        states[1], kept[1][0], cotangent, direct[0:rows] + 0.25 * neighbours(halo=halo)
    )
    cotangent = cotangent + pulls[0]

    direct, mixed = pulled_back(cotangent, wide, kept[0][1], wide_slope_0)
    halo = mixed[0:groups], mixed[groups:close]
    cotangent = adjoint(
        states[0], kept[0][0], cotangent, direct[0:rows] + 0.25 * neighbours(halo=halo)
    )

    final_copy.wait_recv()
    previous = jnp.where(slot == 0, background_ref[...].astype(F32), final_recv[...].astype(F32))
    out_ref[...] = cotangent + error * (control_ref[...] - previous)

    everyone.wait_send()
    for copy in side_copies:
        copy.wait_send()
    for turn in range(steps):
        edge_copy(turn, 0).wait_send()
        edge_copy(turn, 1).wait_send()
    control_copy.wait_send()
    final_copy.wait_send()


def solution(mesh):
    slots, tiles = mesh.shape["slot"], mesh.shape["tile"]

    def per_device(
        control,
        background,
        self_weight,
        neighbour_weight,
        output_weight,
        norm_gain,
        readout,
        error_weight,
        report_owner,
        report_stencil,
        report_weights,
        report_values,
        report_precision,
    ):
        channels = control.shape[-1]
        rows = control.size // channels
        steps = report_values.shape[1]
        groups = rows // BLOCK
        ring = 16 if tiles % 16 == 0 else tiles
        edges = (steps, 2, groups, channels)
        block = (groups, BLOCK, channels)
        message = (tiles, BLOCK, 128)
        operands = (
            control.reshape(rows, channels),
            background.reshape(rows, channels),
            self_weight,
            neighbour_weight,
            output_weight,
            norm_gain.reshape(1, channels),
            readout,
            error_weight.reshape(1, channels),
            report_owner[0].transpose(0, 2, 1),
            report_stencil[0].transpose(0, 2, 1),
            report_weights[0].transpose(0, 2, 1),
            report_values[0],
            report_precision,
        )
        out = pl.pallas_call(
            functools.partial(kernel, slots, tiles, ring, steps),
            out_shape=jax.ShapeDtypeStruct((rows, channels), F32),
            in_specs=[pl.BlockSpec(memory_space=pl.ANY)] * len(operands),
            out_specs=pl.BlockSpec(memory_space=pltpu.VMEM),
            scratch_shapes=[
                *[pltpu.VMEM(operand.shape, operand.dtype) for operand in operands],
                pltpu.SemaphoreType.DMA((len(operands),)),
                pltpu.VMEM((steps, 128, 128), F32),
                pltpu.VMEM(message, BF16),
                pltpu.VMEM(message, BF16),
                pltpu.VMEM(message, F32),
                pltpu.VMEM(edges, BF16),
                pltpu.VMEM(edges, BF16),
                pltpu.VMEM(block, F32),
                pltpu.VMEM(block, F32),
                pltpu.VMEM(block, F32),
                pltpu.VMEM((rows, channels), F32),
                pltpu.VMEM((rows, channels), BF16),
                pltpu.VMEM((rows, channels), BF16),
                pltpu.SemaphoreType.DMA,
                pltpu.SemaphoreType.DMA,
                pltpu.SemaphoreType.DMA((steps, 2)),
                pltpu.SemaphoreType.DMA((steps, 2)),
                pltpu.SemaphoreType.DMA((2,)),
                pltpu.SemaphoreType.DMA((2,)),
                pltpu.VMEM((2, 4 * groups, channels), BF16),
                pltpu.VMEM((2, 4 * groups, channels), BF16),
                pltpu.VMEM((2, 2 * groups, channels), BF16),
                pltpu.VMEM((2, 2 * groups, channels), BF16),
                pltpu.VMEM((2, 3 * groups, 128), BF16),
                pltpu.VMEM((2, 3 * groups, 128), BF16),
                pltpu.VMEM((groups, BLOCK, 128), F32),
                pltpu.SemaphoreType.DMA((3, 2)),
                pltpu.SemaphoreType.DMA((3, 2)),
            ],
            compiler_params=pltpu.CompilerParams(collective_id=0, has_side_effects=True),
        )(*operands)
        return out.reshape(control.shape)

    in_specs = (
        P("slot", None, None, "tile", None),
        P(None, None, "tile", None),
        P(),
        P(),
        P(),
        P(),
        P(),
        P(),
        P("slot", None, "tile", None),
        P("slot", None, "tile", None),
        P("slot", None, "tile", None),
        P("slot", None, "tile", None),
        P("slot", None, "tile"),
    )
    out_specs = P("slot", None, None, "tile", None)
    return jax.shard_map(
        per_device, mesh=mesh, in_specs=in_specs, out_specs=out_specs, check_vma=False
    )
```
